32 devices in a mesh: face: 2 (over x), gx: 4 (over y, core), gy: 4 (over z).
Axes of the slice: x: 2, y: 2, z: 4, core: 2. Of those that a mesh axis runs over, the one named last changes fastest.
Arguments:
- atmos_state: float32 [4, 32, 256, 512], P(None, None, ('face', 'gy'), 'gx'), may hold values from -5 to 5
- atmos_kappa: float32 [256, 512], P(('face', 'gy'), 'gx'), may hold values from 0.05 to 0.24
- ocean_tracers: float32 [2, 32, 256, 512], P(None, None, ('face', 'gy'), 'gx'), may hold values from -5 to 5
- ocean_flow: float32 [2, 32, 256, 512], P(None, None, ('face', 'gy'), 'gx'), may hold values from -0.3 to 0.3
- ocean_kappa: float32 [32, 256, 512], P(None, ('face', 'gy'), 'gx'), may hold values from 0.02 to 0.08
- sea_mask: int32 [256, 512], P(('face', 'gy'), 'gx'), may hold values 0 or 1
- xgrid_atmos_cell: int32 [24, 12, 1024], P(('face', 'gy'), 'gx'), may hold values from 0 to 4095
- xgrid_ocean_cell: int32 [24, 12, 1024], P(('face', 'gy'), 'gx'), may hold values from 0 to 4095
- xgrid_weights: float32 [2, 24, 12, 1024], P(None, ('face', 'gy'), 'gx'), may hold values from 0 to 0.6, as said below
Outputs:
- atmos_next: float32 [4, 32, 256, 512], P(None, None, ('face', 'gy'), 'gx')
- ocean_next: float32 [2, 32, 256, 512], P(None, None, ('face', 'gy'), 'gx')
- ocean_stress: float32 [2, 256, 512], P(None, ('face', 'gy'), 'gx')
The draws below stay inside these ranges and needn't reach their ends.
Inputs may be any that keep to these rules, and one draw needn't show every extreme that they name: `xgrid_weights`: both weights of a slot are zero exactly where the slot carries no intersection and positive elsewhere; within each aligned block of 1024 slots the live ones come first; the run of a block's own offset (a = b = 1) is full, and runs pointing below the first or above the last row of blocks are empty.
All inputs are finite; a program needn't handle non-finite values. No bound on the sum of `sea_mask` on one device may be relied on, other than what follows from the above.
Results may differ from the reference program's by a relative error of at most 0.00002.
Values sent between devices are 32-bit elements; how exact they have to be, the bound alone decides.
A program may use at most 192 MiB of HBM per device.

```python
import math
import jax
import jax.numpy as jnp
from jax import lax

AY = 32
AX = 128
CY = 32
CX = 128
CAP = 1024
LEV_A = 32
LEV_O = 32
ITERS = 24
ATM_SUB = 4
LAT_BLOCKS = 8
LON_BLOCKS = 4
NAY = 256
NAX = 512
NYO = 256
NXO = 512


def live_slots(key):
    counts = jax.random.randint(jax.random.fold_in(key, 7), (LAT_BLOCKS, LON_BLOCKS, 3, 3), CAP // 4, CAP + 1)
    counts = counts.at[:, :, 1, 1].set(CAP)
    block_row = lax.broadcasted_iota(jnp.int32, (LAT_BLOCKS, LON_BLOCKS, 3, 3), 0)
    row_offset = lax.broadcasted_iota(jnp.int32, (LAT_BLOCKS, LON_BLOCKS, 3, 3), 2)
    outside = (block_row == 0) & (row_offset == 0) | (block_row == LAT_BLOCKS - 1) & (row_offset == 2)
    counts = jnp.where(outside, 0, counts)
    slot_index = lax.broadcasted_iota(jnp.int32, (LAT_BLOCKS, LON_BLOCKS, 3, 3, CAP), 4)
    return slot_index < counts[..., None]


def draw_xgrid_weights(key, part):
    live = live_slots(key)
    shape = (2, LAT_BLOCKS, LON_BLOCKS, 3, 3, CAP)
    values = jax.random.uniform(jax.random.fold_in(key, 23), shape, jnp.float32, 0.05, 0.5)
    weights = jnp.where(live[None], values, 0.0).astype(jnp.float32)
    return weights.transpose(0, 1, 3, 2, 4, 5).reshape(2, LAT_BLOCKS * 3, LON_BLOCKS * 3, CAP)


def touch_ends(values, rng, low, high):
    longest = values.shape.index(max(values.shape))
    spots = []
    for shift in (0, 1):
        where = [jax.random.randint(jax.random.fold_in(rng, axis), (), 0, length) for axis, length in enumerate(values.shape)]
        where[longest] = (where[longest] + shift) % values.shape[longest]
        spots.append(tuple(where))
    return values.at[spots[0]].set(low).at[spots[1]].set(high)


def block_scale(key, dims, shards, smallest, high):
    def one(dim, parts):
        draws = jax.random.uniform(jax.random.fold_in(jax.random.fold_in(key, 6), dim), (parts,), jnp.float32, smallest / len(shards), high / len(shards))
        return jnp.repeat(jnp.exp(draws), dims[dim] // parts).reshape((-1,) + (1,) * (len(dims) - dim - 1))

    level = one(*shards[0])
    for cut in shards[1:]:
        level = level * one(*cut)
    return level


def centred(stream_key, extent, scale, limit, shards=(), kind=jnp.bfloat16):
    values = scale * jax.random.normal(stream_key, extent, jnp.float32)
    if shards:
        values = values * block_scale(stream_key, extent, shards, -0.22, 0.18)
    return jnp.clip(values, -limit, limit).astype(kind)


def setup_inputs(seed: int = 0) -> dict:
    splits = jax.random.split(jax.random.key(seed), 10)
    return {
        "atmos_state": centred(splits[0], (4, LEV_A, NAY, NAX), 1.0, 5.0, ((2, 8), (3, 4)), jnp.float32),
        "atmos_kappa": jnp.clip(jnp.exp(math.log(0.24) - 1.5686159 * jax.random.uniform(splits[1], (NAY, NAX), jnp.float32) ** block_scale(splits[1], (NAY, NAX), ((0, 8), (1, 4)), -0.2, 0.2)), 0.05, 0.24),
        "ocean_tracers": centred(splits[2], (2, LEV_O, NYO, NXO), 1.0, 5.0, ((2, 8), (3, 4)), jnp.float32),
        "ocean_flow": jnp.clip(jax.random.uniform(splits[3], (2, LEV_O, NYO, NXO), jnp.float32, -0.3, 0.3) * block_scale(splits[3], (2, LEV_O, NYO, NXO), ((2, 8), (3, 4)), -0.4, 0.0), -0.3, 0.3),
        "ocean_kappa": jnp.clip(jnp.exp(math.log(0.08) - 1.3862944 * jax.random.uniform(splits[4], (LEV_O, NYO, NXO), jnp.float32) ** block_scale(splits[4], (LEV_O, NYO, NXO), ((1, 8), (2, 4)), -0.2, 0.2)), 0.02, 0.08),
        "sea_mask": touch_ends((jax.random.randint(splits[5], (NYO, NXO), 0, 10) < 7).astype(jnp.int32), jax.random.fold_in(splits[5], 1), 0, 1),
        "xgrid_atmos_cell": touch_ends(jax.random.randint(splits[6], (3 * LAT_BLOCKS, 3 * LON_BLOCKS, CAP), 0, AY * AX), jax.random.fold_in(splits[6], 1), 0, (AY * AX) - 1).astype(jnp.int32),
        "xgrid_ocean_cell": touch_ends(jax.random.randint(splits[7], (3 * LAT_BLOCKS, 3 * LON_BLOCKS, CAP), 0, CY * CX), jax.random.fold_in(splits[7], 1), 0, (CY * CX) - 1).astype(jnp.int32),
        "xgrid_weights": draw_xgrid_weights(jax.random.fold_in(splits[9], 71), 0),
    }


current_scale = 2.0
atmos_gain = 0.5
ocean_gain = 0.02

def bulk_fluxes(air_vals, sea_vals):
    temp_air, humid_air, wind_east, wind_north = (air_vals[0], air_vals[1], air_vals[2], air_vals[3])
    sea_temp, current_east, current_north = (sea_vals[0], sea_vals[1], sea_vals[2])
    shear_east = wind_east - current_east
    shear_north = wind_north - current_north
    wind_speed = jnp.sqrt(shear_east * shear_east + shear_north * shear_north + 0.25)
    richardson = (temp_air - sea_temp) / (wind_speed * wind_speed)
    heat_coeff = 0.1 + 0.4 * jax.nn.sigmoid(-2.0 * richardson)
    drag_coeff = 0.2 + 0.1 * jnp.tanh(wind_speed)
    sensible = heat_coeff * wind_speed * (sea_temp - temp_air)
    latent = heat_coeff * wind_speed * (0.5 * jnp.exp(0.3 * sea_temp) - humid_air)
    return jnp.stack([sensible, latent, drag_coeff * wind_speed * shear_east, drag_coeff * wind_speed * shear_north])

def tendency(tracers, west_cells, east_cells, south_cells, north_cells, east_flow, north_flow, diffusion, forcing):
    change = -jnp.maximum(east_flow, 0.0) * (tracers - west_cells) + jnp.maximum(-east_flow, 0.0) * (east_cells - tracers)
    change = change - jnp.maximum(north_flow, 0.0) * (tracers - south_cells) + jnp.maximum(-north_flow, 0.0) * (north_cells - tracers)
    change = change + diffusion * (west_cells + east_cells + south_cells + north_cells - 4.0 * tracers)
    return change.at[:, 0].add(forcing)

def ocean_step(tracers, east_flow, north_flow, diffusion, sea_weight, forcing):
    west_cells = jnp.roll(tracers, 1, axis=3)
    east_cells = jnp.roll(tracers, -1, axis=3)
    south_cells = jnp.concatenate([tracers[:, :, :1], tracers[:, :, :-1]], axis=2)
    north_cells = jnp.concatenate([tracers[:, :, 1:], tracers[:, :, -1:, ::-1]], axis=2)
    change = tendency(tracers, west_cells, east_cells, south_cells, north_cells, east_flow, north_flow, diffusion, forcing)
    return tracers + sea_weight * change

def reference(atmos_state, atmos_kappa, ocean_tracers, ocean_flow, ocean_kappa, sea_mask, xgrid_atmos_cell, xgrid_ocean_cell, xgrid_weights):
    lat_count = LAT_BLOCKS
    lon_count = LON_BLOCKS
    atmos_cells = AY * AX
    ocean_cells = CY * CX
    lowest = atmos_state[:, 0].reshape(4, lat_count, AY, lon_count, AX).transpose(0, 1, 3, 2, 4).reshape(4, lat_count, lon_count, atmos_cells)
    surface = jnp.stack([ocean_tracers[0, 0], current_scale * ocean_flow[0, 0], current_scale * ocean_flow[1, 0]])
    surface = surface.reshape(3, lat_count, CY, lon_count, CX).transpose(0, 1, 3, 2, 4).reshape(3, lat_count, lon_count, ocean_cells)
    atmos_index = xgrid_atmos_cell.reshape(lat_count, 3, lon_count, 3, CAP)
    ocean_index = xgrid_ocean_cell.reshape(lat_count, 3, lon_count, 3, CAP)
    weights = xgrid_weights.reshape(2, lat_count, 3, lon_count, 3, CAP)
    row_index = lax.broadcasted_iota(jnp.int32, (lat_count, lon_count, CAP), 0)
    col_index = lax.broadcasted_iota(jnp.int32, (lat_count, lon_count, CAP), 1)
    atmos_flux = jnp.zeros((4, lat_count * lon_count * atmos_cells), jnp.float32)
    ocean_flux = jnp.zeros((4, lat_count * lon_count * ocean_cells), jnp.float32)
    for row_off in range(3):
        for col_off in range(3):
            atmos_pick = atmos_index[:, row_off, :, col_off]
            ocean_pick = ocean_index[:, row_off, :, col_off]
            air_vals = jnp.take_along_axis(lowest, atmos_pick[None], axis=3)
            shifted = jnp.roll(surface, (1 - row_off, 1 - col_off), axis=(1, 2))
            sea_vals = jnp.take_along_axis(shifted, ocean_pick[None], axis=3)
            fluxes = bulk_fluxes(air_vals, sea_vals)
            atmos_place = ((row_index * lon_count + col_index) * atmos_cells + atmos_pick).reshape(-1).astype(jnp.int32)
            atmos_flux = atmos_flux.at[:, atmos_place].add((weights[0][:, row_off, :, col_off] * fluxes).reshape(4, -1))
            ocean_row = (row_index + (row_off - 1)) % lat_count
            ocean_col = (col_index + (col_off - 1)) % lon_count
            ocean_place = ((ocean_row * lon_count + ocean_col) * ocean_cells + ocean_pick).reshape(-1).astype(jnp.int32)
            ocean_flux = ocean_flux.at[:, ocean_place].add((weights[1][:, row_off, :, col_off] * fluxes).reshape(4, -1))
    atmos_flux = atmos_flux.reshape(4, lat_count, lon_count, AY, AX).transpose(0, 1, 3, 2, 4).reshape(4, lat_count * AY, lon_count * AX)
    ocean_flux = ocean_flux.reshape(4, lat_count, lon_count, CY, CX).transpose(0, 1, 3, 2, 4).reshape(4, lat_count * CY, lon_count * CX)
    flux_gains = jnp.array([atmos_gain, atmos_gain, -atmos_gain, -atmos_gain], jnp.float32)
    atmos_now = atmos_state.at[:, 0].add(flux_gains[:, None, None] * atmos_flux)
    for _ in range(ATM_SUB):
        above_cells = jnp.concatenate([atmos_now[:, 1:], atmos_now[:, -1:]], axis=1)
        below_cells = jnp.concatenate([atmos_now[:, :1], atmos_now[:, :-1]], axis=1)
        atmos_now = atmos_now + atmos_kappa * (above_cells + below_cells - 2.0 * atmos_now)
    sea_weight = sea_mask.astype(jnp.float32)
    forcing = jnp.stack([-ocean_gain * (ocean_flux[0] + ocean_flux[1]), ocean_gain * ocean_flux[1]])

    def advance(iteration, tracers):
        return ocean_step(tracers, ocean_flow[0], ocean_flow[1], ocean_kappa, sea_weight, forcing)
    ocean_now = lax.fori_loop(0, ITERS, advance, ocean_tracers)
    ocean_stress = sea_weight * ocean_flux[2:4]
    return (atmos_now, ocean_now, ocean_stress)
```

```python
import functools

import jax
import jax.numpy as jnp
from jax import lax
from jax.experimental import pallas as pl
from jax.experimental.pallas import tpu as pltpu
from jax.sharding import PartitionSpec as P

ITERS = 24
ATM_SUB = 4
DEPTH = 8

current_scale = 2.0
atmos_gain = 0.5
ocean_gain = 0.02
MESH = pl.DeviceIdType.MESH
F32 = jnp.float32
BF16 = jnp.bfloat16


def bulk_fluxes(air_vals, sea_vals):
    temp_air, humid_air, wind_east, wind_north = air_vals
    sea_temp, current_east, current_north = sea_vals
    shear_east = wind_east - current_east
    shear_north = wind_north - current_north
    wind_speed = jnp.sqrt(shear_east * shear_east + shear_north * shear_north + 0.25)
    richardson = (temp_air - sea_temp) / (wind_speed * wind_speed)
    heat_coeff = 0.1 + 0.4 * jax.nn.sigmoid(-2.0 * richardson)
    drag_coeff = 0.2 + 0.1 * jnp.tanh(wind_speed)
    sensible = heat_coeff * wind_speed * (sea_temp - temp_air)
    latent = heat_coeff * wind_speed * (0.5 * jnp.exp(0.3 * sea_temp) - humid_air)
    return [
        sensible,
        latent,
        drag_coeff * wind_speed * shear_east,
        drag_coeff * wind_speed * shear_north,
    ]


def pieces(value):
    parts = []
    for _ in range(3):
        part = value.astype(BF16)
        parts.append(part)
        value = value - part.astype(F32)
    return parts


def pick(table, onehot_col, onehot_row, rows, fields):
    total = None
    for part in pieces(table):
        term = lax.dot_general(part, onehot_col, (((1,), (0,)), ((), ())), preferred_element_type=F32)
        total = term if total is None else total + term
    return [
        jnp.sum(jnp.where(onehot_row, total[f * rows : (f + 1) * rows], 0.0), axis=0, keepdims=True)
        for f in range(fields)
    ]


def place(values, onehot_col, onehot_row):
    split = [pieces(value) for value in values]
    total = None
    for k in range(3):
        spread = jnp.concatenate(
            [jnp.where(onehot_row, part[k].astype(F32), 0.0) for part in split], axis=0
        ).astype(BF16)
        term = lax.dot_general(spread, onehot_col, (((1,), (1,)), ((), ())), preferred_element_type=F32)
        total = term if total is None else total + term
    return total


def xgrid_kernel(low_ref, near_ref, acell_ref, ocell_ref, w_ref, aflux_ref, oflux_ref, *, rows, cols):
    slots = acell_ref.shape[2]
    bits = cols.bit_length() - 1
    col_iota = lax.broadcasted_iota(jnp.int32, (cols, slots), 0)
    row_iota = lax.broadcasted_iota(jnp.int32, (rows, slots), 0)

    def hots(cell):
        col = jnp.where(col_iota == (cell & (cols - 1)), 1.0, 0.0).astype(BF16)
        return col, row_iota == (cell >> bits)

    acol, arow = hots(acell_ref[0])
    ocol, orow = hots(ocell_ref[0])
    air = pick(low_ref[...], acol, arow, rows, 4)
    sea = pick(near_ref[0], ocol, orow, rows, 3)
    fluxes = bulk_fluxes(air, sea)
    weight_air = w_ref[0, 0]
    weight_sea = w_ref[1, 0]
    mine = place([weight_air * flux for flux in fluxes], acol, arow)

    @pl.when(pl.program_id(0) == 0)
    def _():
        aflux_ref[...] = mine

    @pl.when(pl.program_id(0) > 0)
    def _():
        aflux_ref[...] += mine

    oflux_ref[0] = place([weight_sea * flux for flux in fluxes], ocol, orow)


def xgrid(lowest, nearby, acell, ocell, weights, rows, cols):
    count, _, slots = acell.shape
    return pl.pallas_call(
        functools.partial(xgrid_kernel, rows=rows, cols=cols),
        grid=(count,),
        in_specs=[
            pl.BlockSpec((4 * rows, cols), lambda j: (0, 0)),
            pl.BlockSpec((1, 3 * rows, cols), lambda j: (j, 0, 0)),
            pl.BlockSpec((1, 1, slots), lambda j: (j, 0, 0)),
            pl.BlockSpec((1, 1, slots), lambda j: (j, 0, 0)),
            pl.BlockSpec((2, 1, 1, slots), lambda j: (0, j, 0, 0)),
        ],
        out_specs=[
            pl.BlockSpec((4 * rows, cols), lambda j: (0, 0)),
            pl.BlockSpec((1, 4 * rows, cols), lambda j: (j, 0, 0)),
        ],
        out_shape=[
            jax.ShapeDtypeStruct((4 * rows, cols), F32),
            jax.ShapeDtypeStruct((count, 4 * rows, cols), F32),
        ],
        name="xgrid",
    )(lowest, nearby, acell, ocell, weights)


def atmos_kernel(state_ref, kappa_ref, flux_ref, out_ref):
    levels, rows = state_ref.shape[1], state_ref.shape[2]
    gain = jnp.where(pl.program_id(0) < 2, atmos_gain, -atmos_gain)
    for tile in range(rows // 8):
        at = slice(tile * 8, tile * 8 + 8)
        kappa = kappa_ref[at, :]
        now = [state_ref[0, level, at, :] for level in range(levels)]
        now[0] = now[0] + gain * flux_ref[0, at, :]
        for _ in range(ATM_SUB):
            now = [
                now[l] + kappa * (now[min(l + 1, levels - 1)] + now[max(l - 1, 0)] - 2.0 * now[l])
                for l in range(levels)
            ]
        for level in range(levels):
            out_ref[0, level, at, :] = now[level]


def atmosphere(state, kappa, flux):
    fields, levels, rows, cols = state.shape
    return pl.pallas_call(
        atmos_kernel,
        grid=(fields,),
        in_specs=[
            pl.BlockSpec((1, levels, rows, cols), lambda f: (f, 0, 0, 0)),
            pl.BlockSpec((rows, cols), lambda f: (0, 0)),
            pl.BlockSpec((1, rows, cols), lambda f: (f, 0, 0)),
        ],
        out_specs=pl.BlockSpec((1, levels, rows, cols), lambda f: (f, 0, 0, 0)),
        out_shape=jax.ShapeDtypeStruct(state.shape, F32),
        name="atmosphere",
    )(state, kappa, flux)


def flipped(value, sign):
    rows, cols = value.shape
    for axis, size in ((1, cols), (0, rows)):
        index = lax.broadcasted_iota(jnp.int32, value.shape, axis)
        bit = 1
        while bit < size:
            up = pltpu.roll(value, bit, axis)
            down = pltpu.roll(value, size - bit, axis)
            value = jnp.where((index & bit) == 0, down, up)
            bit *= 2
    return value * sign


def ocean_kernel(
    tr_ref, fl_ref, ka_ref, mask_ref, flux_ref, out_ref,
    st, halo, xt, send_e, send_w, recv_w, recv_e, coef_c, coef_x, force_c, force_x,
    row_send, row_recv, col_send, col_recv,
    *, lat_axes, face_count, gy_count, gx_count,
):
    levels, rows, cols = tr_ref.shape[1], tr_ref.shape[2], tr_ref.shape[3]
    depth = DEPTH
    tall = rows + 2 * depth
    per = cols // depth
    rounds = ITERS // depth
    dyn = 2 * levels
    mask_at = dyn + 3 * levels
    used = mask_at + 3
    groups_all = st.shape[0] // per
    groups_dyn = dyn // per

    face, gy, gx = lax.axis_index("face"), lax.axis_index("gy"), lax.axis_index("gx")
    pos = face * gy_count + gy
    last = face_count * gy_count - 1
    top = pos == last
    n_pos = jnp.where(top, pos, pos + 1)
    n_gx = jnp.where(top, gx_count - 1 - gx, gx)
    s_pos = jnp.where(pos > 0, pos - 1, 0)
    north = {"face": n_pos // gy_count, "gx": n_gx, "gy": n_pos % gy_count}
    south = {"face": s_pos // gy_count, "gx": gx, "gy": s_pos % gy_count}
    east = {"face": face, "gx": (gx + 1) % gx_count, "gy": gy}
    west = {"face": face, "gx": (gx + gx_count - 1) % gx_count, "gy": gy}
    n_slot = jnp.where(top, 1, 0)

    barrier = pltpu.get_barrier_semaphore()
    for where in (north, east, west):
        pl.semaphore_signal(barrier, inc=1, device_id=where, device_id_type=MESH)

    @pl.when(pos > 0)
    def _():
        pl.semaphore_signal(barrier, inc=1, device_id=south, device_id_type=MESH)

    def fill(l, _):
        for t in range(2):
            st[t * levels + l] = tr_ref[t, l]
            st[dyn + t * levels + l] = fl_ref[t, l]
        st[dyn + 2 * levels + l] = ka_ref[l]
        return 0

    lax.fori_loop(0, levels, fill, 0)
    st[mask_at] = mask_ref[...]
    st[mask_at + 1] = -ocean_gain * (flux_ref[0] + flux_ref[1])
    st[mask_at + 2] = ocean_gain * flux_ref[1]
    for plane in range(used, st.shape[0]):
        st[plane] = jnp.zeros((rows, cols), F32)
        for e in range(rounds):
            for s in range(2):
                halo[e, s, plane] = jnp.zeros((depth, cols), F32)

    @pl.when(pos == 0)
    def _():
        def clear(plane, _):
            for e in range(rounds):
                halo[e, 0, plane] = jnp.zeros((depth, cols), F32)
            return 0

        lax.fori_loop(0, used, clear, 0)

    pl.semaphore_wait(barrier, jnp.where(pos > 0, 4, 3))

    lane = lax.broadcasted_iota(jnp.int32, (tall, cols), 1)
    slot = lane // depth

    def column(e, plane):
        return jnp.concatenate([halo[e, 0, plane], st[plane], halo[e, 1, plane]], axis=0)

    def exchange(e, planes, groups):
        up = pltpu.make_async_remote_copy(
            src_ref=st.at[pl.ds(0, planes), pl.ds(rows - depth, depth), :],
            dst_ref=halo.at[e, n_slot, pl.ds(0, planes)],
            send_sem=row_send.at[e, 0], recv_sem=row_recv.at[e, n_slot],
            device_id=north, device_id_type=MESH,
        )
        down = pltpu.make_async_remote_copy(
            src_ref=st.at[pl.ds(0, planes), pl.ds(0, depth), :],
            dst_ref=halo.at[e, 1, pl.ds(0, planes)],
            send_sem=row_send.at[e, 1], recv_sem=row_recv.at[e, 1],
            device_id=south, device_id_type=MESH,
        )
        from_south = pltpu.make_async_remote_copy(
            src_ref=st.at[pl.ds(0, planes), pl.ds(0, depth), :],
            dst_ref=halo.at[e, 0, pl.ds(0, planes)],
            send_sem=row_send.at[e, 1], recv_sem=row_recv.at[e, 0],
            device_id=south, device_id_type=MESH,
        )
        up.start()

        @pl.when(pos > 0)
        def _():
            down.start()
            from_south.wait_recv()
            down.wait_send()

        down.wait_recv()
        up.wait_send()

        @pl.when(top)
        def _():
            def turn(plane, _):
                backward = jnp.logical_and(plane >= dyn, plane < dyn + 2 * levels)
                halo[e, 1, plane] = flipped(halo[e, 1, plane], jnp.where(backward, -1.0, 1.0))
                return 0

            lax.fori_loop(0, planes, turn, 0)

        def pack(g, _):
            to_east = jnp.zeros((tall, cols), F32)
            to_west = jnp.zeros((tall, cols), F32)
            for p in range(per):
                value = column(e, g * per + p)
                here = slot == p
                shift_e = (p + 1) * depth % cols
                moved_e = pltpu.roll(value, shift_e, 1) if shift_e else value
                moved_w = pltpu.roll(value, p * depth, 1) if p else value
                to_east = jnp.where(here, moved_e, to_east)
                to_west = jnp.where(here, moved_w, to_west)
            send_e[e, g] = to_east
            send_w[e, g] = to_west
            return 0

        lax.fori_loop(0, groups, pack, 0)
        go_e = pltpu.make_async_remote_copy(
            src_ref=send_e.at[e, pl.ds(0, groups)], dst_ref=recv_w.at[e, pl.ds(0, groups)],
            send_sem=col_send.at[e, 0], recv_sem=col_recv.at[e, 0],
            device_id=east, device_id_type=MESH,
        )
        go_w = pltpu.make_async_remote_copy(
            src_ref=send_w.at[e, pl.ds(0, groups)], dst_ref=recv_e.at[e, pl.ds(0, groups)],
            send_sem=col_send.at[e, 1], recv_sem=col_recv.at[e, 1],
            device_id=west, device_id_type=MESH,
        )
        go_e.start()
        go_w.start()
        go_e.wait()
        go_w.wait()

        def unpack(g, _):
            for p in range(per):
                from_e = recv_e[e, g]
                from_w = recv_w[e, g]
                shift_w = (cols - depth - p * depth) % cols
                low = pltpu.roll(from_e, cols - p * depth, 1) if p else from_e
                high = pltpu.roll(from_w, shift_w, 1) if shift_w else from_w
                xt[g * per + p] = jnp.where(slot == 0, low, jnp.where(slot == per - 1, high, 0.0))
            return 0

        lax.fori_loop(0, groups, unpack, 0)

    exchange(0, used, groups_all)

    row_index = lax.broadcasted_iota(jnp.int32, (tall, cols), 0)
    floor = jnp.logical_and(row_index == depth, pos == 0)

    def weights(get, out):
        mask = get(mask_at)

        def one(l, _):
            u, v, k = get(dyn + l), get(dyn + levels + l), get(dyn + 2 * levels + l)
            w = mask * (jnp.maximum(u, 0.0) + k)
            e = mask * (jnp.maximum(-u, 0.0) + k)
            s = jnp.where(floor, 0.0, mask * (jnp.maximum(v, 0.0) + k))
            n = mask * (jnp.maximum(-v, 0.0) + k)
            out[0, l] = 1.0 - ((w + e) + (s + n))
            out[1, l] = w
            out[2, l] = e
            out[3, l] = s
            out[4, l] = n
            return 0

        lax.fori_loop(0, levels, one, 0)
        return mask

    centre = functools.partial(column, 0)
    mask_c = weights(centre, coef_c)
    mask_x = weights(lambda plane: xt[plane], coef_x)
    for t in range(2):
        force_c[t] = mask_c * centre(mask_at + 1 + t)
        force_x[t] = mask_x * xt[mask_at + 1 + t]

    first = lane == 0
    final = lane == cols - 1

    def advance(e, l, forced):
        now = [(column(e, t * levels + l), xt[t * levels + l]) for t in range(2)]
        for _ in range(depth):
            later = []
            for t in range(2):
                c, x = now[t]
                rc, rx = pltpu.roll(c, 1, 1), pltpu.roll(x, 1, 1)
                lc, lx = pltpu.roll(c, cols - 1, 1), pltpu.roll(x, cols - 1, 1)
                pair = []
                for mine, w, ea, coef, force in (
                    (c, jnp.where(first, rx, rc), jnp.where(final, lx, lc), coef_c, force_c),
                    (x, jnp.where(first, rc, rx), jnp.where(final, lc, lx), coef_x, force_x),
                ):
                    so = pltpu.roll(mine, 1, 0)
                    no = pltpu.roll(mine, tall - 1, 0)
                    new = coef[0, l] * mine + (coef[1, l] * w + coef[2, l] * ea)
                    new = new + (coef[3, l] * so + coef[4, l] * no)
                    pair.append(new + force[t] if forced else new)
                later.append(tuple(pair))
            now = later
        for t in range(2):
            st[t * levels + l] = now[t][0][depth : depth + rows]

    def round_of(e, _):
        advance(e, 0, True)

        def level(l, _):
            advance(e, l, False)
            return 0

        lax.fori_loop(1, levels, level, 0)

        @pl.when(e < rounds - 1)
        def _():
            exchange(e + 1, dyn, groups_dyn)

        return 0

    lax.fori_loop(0, rounds, round_of, 0)

    def empty(l, _):
        for t in range(2):
            out_ref[t, l] = st[t * levels + l]
        return 0

    lax.fori_loop(0, levels, empty, 0)


def ocean(tracers, flow, kappa, mask, flux):
    _, levels, rows, cols = tracers.shape
    depth = DEPTH
    tall = rows + 2 * depth
    per = cols // depth
    rounds = ITERS // depth
    groups = -(-(5 * levels + 3) // per)
    planes = groups * per
    vm = lambda *shape: pltpu.VMEM(shape, F32)
    return pl.pallas_call(
        functools.partial(
            ocean_kernel, lat_axes=("face", "gy"), face_count=lax.axis_size("face"),
            gy_count=lax.axis_size("gy"), gx_count=lax.axis_size("gx"),
        ),
        in_specs=[pl.BlockSpec(memory_space=pltpu.VMEM)] * 5,
        out_specs=pl.BlockSpec(memory_space=pltpu.VMEM),
        out_shape=jax.ShapeDtypeStruct(tracers.shape, F32),
        scratch_shapes=[
            vm(planes, rows, cols),
            vm(rounds, 2, planes, depth, cols),
            vm(planes, tall, cols),
            vm(rounds, groups, tall, cols),
            vm(rounds, groups, tall, cols),
            vm(rounds, groups, tall, cols),
            vm(rounds, groups, tall, cols),
            vm(5, levels, tall, cols),
            vm(5, levels, tall, cols),
            vm(2, tall, cols),
            vm(2, tall, cols),
            pltpu.SemaphoreType.DMA((rounds, 2)),
            pltpu.SemaphoreType.DMA((rounds, 2)),
            pltpu.SemaphoreType.DMA((rounds, 2)),
            pltpu.SemaphoreType.DMA((rounds, 2)),
        ],
        compiler_params=pltpu.CompilerParams(
            collective_id=0, has_side_effects=True, vmem_limit_bytes=56 * 1024 * 1024
        ),
        name="ocean",
    )(tracers, flow, kappa, mask, flux)


def shifted(value, axis, step, wrap):
    count = lax.axis_size(axis)
    pairs = [(i, (i + step) % count) for i in range(count) if wrap or 0 <= i + step < count]
    return lax.ppermute(value, axis, pairs)


def local(
    atmos_state, atmos_kappa, ocean_tracers, ocean_flow, ocean_kappa, sea_mask,
    xgrid_atmos_cell, xgrid_ocean_cell, xgrid_weights,
):
    rows, cols = ocean_tracers.shape[2], ocean_tracers.shape[3]
    slots = xgrid_atmos_cell.shape[2]
    lat = ("face", "gy")
    lowest = atmos_state[:, 0].reshape(-1, cols)
    surface = jnp.concatenate(
        [ocean_tracers[0, 0], current_scale * ocean_flow[0, 0], current_scale * ocean_flow[1, 0]]
    )[None]
    tall = jnp.concatenate(
        [shifted(surface, lat, 1, False), surface, shifted(surface, lat, -1, False)]
    )
    nearby = jnp.stack([shifted(tall, "gx", 1, True), tall, shifted(tall, "gx", -1, True)], axis=1)
    atmos_flux, blocks = xgrid(
        lowest,
        nearby.reshape(9, 3 * rows, cols),
        xgrid_atmos_cell.reshape(9, 1, slots),
        xgrid_ocean_cell.reshape(9, 1, slots),
        xgrid_weights.reshape(2, 9, 1, slots),
        rows, cols,
    )
    blocks = blocks.reshape(3, 3, 4, rows, cols)
    middle = (
        blocks[1] + shifted(blocks[2], lat, 1, False) + shifted(blocks[0], lat, -1, False)
    )
    ocean_flux = (
        middle[1] + shifted(middle[2], "gx", 1, True) + shifted(middle[0], "gx", -1, True)
    )
    atmos_now = atmosphere(atmos_state, atmos_kappa, atmos_flux.reshape(4, rows, cols))
    sea_weight = sea_mask.astype(F32)
    ocean_now = ocean(ocean_tracers, ocean_flow, ocean_kappa, sea_weight, ocean_flux)
    return (atmos_now, ocean_now, sea_weight * ocean_flux[2:4])


def solution(mesh):
    placed = (
        P(None, None, ("face", "gy"), "gx"),
        P(("face", "gy"), "gx"),
        P(None, None, ("face", "gy"), "gx"),
        P(None, None, ("face", "gy"), "gx"),
        P(None, ("face", "gy"), "gx"),
        P(("face", "gy"), "gx"),
        P(("face", "gy"), "gx", None),
        P(("face", "gy"), "gx", None),
        P(None, ("face", "gy"), "gx", None),
    )
    return jax.shard_map(
        local,
        mesh=mesh,
        in_specs=placed,
        out_specs=(
            P(None, None, ("face", "gy"), "gx"),
            P(None, None, ("face", "gy"), "gx"),
            P(None, ("face", "gy"), "gx"),
        ),
        check_vma=False,
    )
```

```python
import functools

import jax
import jax.numpy as jnp
from jax import lax
from jax.experimental import pallas as pl
from jax.experimental.pallas import tpu as pltpu
from jax.sharding import PartitionSpec as P

ITERS = 24
ATM_SUB = 4
DEPTH = 8

current_scale = 2.0
atmos_gain = 0.5
ocean_gain = 0.02
MESH = pl.DeviceIdType.MESH
F32 = jnp.float32
BF16 = jnp.bfloat16


def bulk_fluxes(air_vals, sea_vals):
    temp_air, humid_air, wind_east, wind_north = air_vals
    sea_temp, current_east, current_north = sea_vals
    shear_east = wind_east - current_east
    shear_north = wind_north - current_north
    wind_speed = jnp.sqrt(shear_east * shear_east + shear_north * shear_north + 0.25)
    richardson = (temp_air - sea_temp) / (wind_speed * wind_speed)
    heat_coeff = 0.1 + 0.4 * jax.nn.sigmoid(-2.0 * richardson)
    drag_coeff = 0.2 + 0.1 * jnp.tanh(wind_speed)
    sensible = heat_coeff * wind_speed * (sea_temp - temp_air)
    latent = heat_coeff * wind_speed * (0.5 * jnp.exp(0.3 * sea_temp) - humid_air)
    return [
        sensible,
        latent,
        drag_coeff * wind_speed * shear_east,
        drag_coeff * wind_speed * shear_north,
    ]


def pieces(value):
    parts = []
    for _ in range(3):
        part = value.astype(BF16)
        parts.append(part)
        value = value - part.astype(F32)
    return parts


def pick(table, onehot_col, onehot_row, rows, fields):
    total = None
    for part in pieces(table):
        term = lax.dot_general(part, onehot_col, (((1,), (0,)), ((), ())), preferred_element_type=F32)
        total = term if total is None else total + term
    return [
        jnp.sum(jnp.where(onehot_row, total[f * rows : (f + 1) * rows], 0.0), axis=0, keepdims=True)
        for f in range(fields)
    ]


def place(values, onehot_col, onehot_row):
    split = [pieces(value) for value in values]
    total = None
    for k in range(3):
        spread = jnp.concatenate(
            [jnp.where(onehot_row, part[k].astype(F32), 0.0) for part in split], axis=0
        ).astype(BF16)
        term = lax.dot_general(spread, onehot_col, (((1,), (1,)), ((), ())), preferred_element_type=F32)
        total = term if total is None else total + term
    return total


def xgrid_kernel(low_ref, near_ref, acell_ref, ocell_ref, w_ref, aflux_ref, oflux_ref, *, rows, cols):
    slots = acell_ref.shape[2]
    bits = cols.bit_length() - 1
    col_iota = lax.broadcasted_iota(jnp.int32, (cols, slots), 0)
    row_iota = lax.broadcasted_iota(jnp.int32, (rows, slots), 0)

    def hots(cell):
        col = jnp.where(col_iota == (cell & (cols - 1)), 1.0, 0.0).astype(BF16)
        return col, row_iota == (cell >> bits)

    acol, arow = hots(acell_ref[0])
    ocol, orow = hots(ocell_ref[0])
    air = pick(low_ref[...], acol, arow, rows, 4)
    sea = pick(near_ref[0], ocol, orow, rows, 3)
    fluxes = bulk_fluxes(air, sea)
    weight_air = w_ref[0, 0]
    weight_sea = w_ref[1, 0]
    mine = place([weight_air * flux for flux in fluxes], acol, arow)

    @pl.when(pl.program_id(0) == 0)
    def _():
        aflux_ref[...] = mine

    @pl.when(pl.program_id(0) > 0)
    def _():
        aflux_ref[...] += mine

    oflux_ref[0] = place([weight_sea * flux for flux in fluxes], ocol, orow)


def xgrid(lowest, nearby, acell, ocell, weights, rows, cols):
    count, _, slots = acell.shape
    return pl.pallas_call(
        functools.partial(xgrid_kernel, rows=rows, cols=cols),
        grid=(count,),
        in_specs=[
            pl.BlockSpec((4 * rows, cols), lambda j: (0, 0)),
            pl.BlockSpec((1, 3 * rows, cols), lambda j: (j, 0, 0)),
            pl.BlockSpec((1, 1, slots), lambda j: (j, 0, 0)),
            pl.BlockSpec((1, 1, slots), lambda j: (j, 0, 0)),
            pl.BlockSpec((2, 1, 1, slots), lambda j: (0, j, 0, 0)),
        ],
        out_specs=[
            pl.BlockSpec((4 * rows, cols), lambda j: (0, 0)),
            pl.BlockSpec((1, 4 * rows, cols), lambda j: (j, 0, 0)),
        ],
        out_shape=[
            jax.ShapeDtypeStruct((4 * rows, cols), F32),
            jax.ShapeDtypeStruct((count, 4 * rows, cols), F32),
        ],
        name="xgrid",
    )(lowest, nearby, acell, ocell, weights)


def atmos_kernel(state_ref, kappa_ref, flux_ref, out_ref):
    levels, rows = state_ref.shape[1], state_ref.shape[2]
    gain = jnp.where(pl.program_id(0) < 2, atmos_gain, -atmos_gain)
    for tile in range(rows // 8):
        at = slice(tile * 8, tile * 8 + 8)
        kappa = kappa_ref[at, :]
        now = [state_ref[0, level, at, :] for level in range(levels)]
        now[0] = now[0] + gain * flux_ref[0, at, :]
        for _ in range(ATM_SUB):
            now = [
                now[l] + kappa * (now[min(l + 1, levels - 1)] + now[max(l - 1, 0)] - 2.0 * now[l])
                for l in range(levels)
            ]
        for level in range(levels):
            out_ref[0, level, at, :] = now[level]


def atmosphere(state, kappa, flux):
    fields, levels, rows, cols = state.shape
    return pl.pallas_call(
        atmos_kernel,
        grid=(fields,),
        in_specs=[
            pl.BlockSpec((1, levels, rows, cols), lambda f: (f, 0, 0, 0)),
            pl.BlockSpec((rows, cols), lambda f: (0, 0)),
            pl.BlockSpec((1, rows, cols), lambda f: (f, 0, 0)),
        ],
        out_specs=pl.BlockSpec((1, levels, rows, cols), lambda f: (f, 0, 0, 0)),
        out_shape=jax.ShapeDtypeStruct(state.shape, F32),
        name="atmosphere",
    )(state, kappa, flux)


def mirror(value):
    cols = value.shape[1]
    row = lax.broadcasted_iota(jnp.int32, (cols, cols), 0)
    col = lax.broadcasted_iota(jnp.int32, (cols, cols), 1)
    swap = jnp.where(row + col == cols - 1, 1.0, 0.0).astype(BF16)
    total = None
    for part in pieces(value):
        term = jnp.dot(part, swap, preferred_element_type=F32)
        total = term if total is None else total + term
    return total


def ocean_kernel(
    all_ref, misc_ref, st,
    halo0, halo_m, halo1, send0, recv0, send1, recv1, xt0, ping, pong, coef, force,
    row0_send, row0_recv, misc_send, misc_recv, col0_send, col0_recv,
    row_send, row_recv, col_send, col_recv,
    *, face_count, gy_count, gx_count,
):
    rows, groups, sub, cols = all_ref.shape
    chunks = groups // 5
    depth = DEPTH
    tall = rows + 2 * depth
    per = cols // depth
    packs = tall // per
    rounds = ITERS // depth
    end = depth + rows

    face, gy, gx = lax.axis_index("face"), lax.axis_index("gy"), lax.axis_index("gx")
    pos = face * gy_count + gy
    last = face_count * gy_count - 1
    top = pos == last
    n_pos = jnp.where(top, pos, pos + 1)
    n_gx = jnp.where(top, gx_count - 1 - gx, gx)
    s_pos = jnp.where(pos > 0, pos - 1, 0)
    north = {"face": n_pos // gy_count, "gx": n_gx, "gy": n_pos % gy_count}
    south = {"face": s_pos // gy_count, "gx": gx, "gy": s_pos % gy_count}
    east = {"face": face, "gx": (gx + 1) % gx_count, "gy": gy}
    west = {"face": face, "gx": (gx + gx_count - 1) % gx_count, "gy": gy}
    n_slot = jnp.where(top, 1, 0)

    barrier = pltpu.get_barrier_semaphore()
    for where in (north, east, west):
        pl.semaphore_signal(barrier, inc=1, device_id=where, device_id_type=MESH)

    @pl.when(pos > 0)
    def _():
        pl.semaphore_signal(barrier, inc=1, device_id=south, device_id_type=MESH)

    @pl.when(pos == 0)
    def _():
        def clear(r, _):
            halo0[0, r] = jnp.zeros((groups, sub, cols), F32)
            halo_m[0, r] = jnp.zeros((sub, cols), F32)
            for e in range(rounds - 1):
                for c in range(chunks):
                    halo1[e, c, 0, r] = jnp.zeros((2, sub, cols), F32)
            return 0

        lax.fori_loop(0, depth, clear, 0)

    pl.semaphore_wait(barrier, jnp.where(pos > 0, 4, 3))

    def remote(src, dst, send, recv, device):
        return pltpu.make_async_remote_copy(
            src_ref=src, dst_ref=dst, send_sem=send, recv_sem=recv,
            device_id=device, device_id_type=MESH,
        )

    def row_copies(high, low, halo_of, send, recv):
        up = remote(high, halo_of(n_slot), send(0), recv(n_slot), north)
        down = remote(low, halo_of(1), send(1), recv(1), south)
        below = remote(low, halo_of(0), send(1), recv(0), south)
        return up, down, below

    def begin(copies):
        copies[0].start()

        @pl.when(pos > 0)
        def _():
            copies[1].start()

    def finish(copies):
        up, down, below = copies

        @pl.when(pos > 0)
        def _():
            below.wait_recv()
            down.wait_send()

        down.wait_recv()
        up.wait_send()

    lane = lax.broadcasted_iota(jnp.int32, (sub, cols), 1)
    slot = lane // depth
    first = lane == 0
    final = lane == cols - 1

    def packed(value_of):
        to_east, to_west = None, None
        for p in range(per):
            value = value_of(p)
            shift_e = (p + 1) * depth % cols
            moved_e = pltpu.roll(value, shift_e, 1) if shift_e else value
            moved_w = pltpu.roll(value, p * depth, 1) if p else value
            to_east = moved_e if p == 0 else jnp.where(slot == p, moved_e, to_east)
            to_west = moved_w if p == 0 else jnp.where(slot == p, moved_w, to_west)
        return to_east, to_west

    def unpacked(from_w, from_e, p):
        shift_w = (cols - depth - p * depth) % cols
        low = pltpu.roll(from_e, cols - p * depth, 1) if p else from_e
        high = pltpu.roll(from_w, shift_w, 1) if shift_w else from_w
        return jnp.where(slot == 0, low, jnp.where(slot == per - 1, high, 0.0))

    rows0 = row_copies(
        all_ref.at[pl.ds(rows - depth, depth)], all_ref.at[pl.ds(0, depth)],
        lambda s: halo0.at[s], lambda s: row0_send.at[s], lambda s: row0_recv.at[s],
    )
    rows_m = row_copies(
        misc_ref.at[pl.ds(rows - depth, depth)], misc_ref.at[pl.ds(0, depth)],
        lambda s: halo_m.at[s], lambda s: misc_send.at[s], lambda s: misc_recv.at[s],
    )
    begin(rows0)
    begin(rows_m)
    finish(rows0)
    finish(rows_m)

    @pl.when(top)
    def _():
        kind = (lax.broadcasted_iota(jnp.int32, (groups * sub, cols), 0) // sub) % 5
        sign = jnp.where(jnp.logical_or(kind == 2, kind == 3), -1.0, 1.0)

        def turn(i, _):
            j = depth - 1 - i
            a = mirror(halo0[1, i].reshape(groups * sub, cols)) * sign
            b = mirror(halo0[1, j].reshape(groups * sub, cols)) * sign
            halo0[1, i] = b.reshape(groups, sub, cols)
            halo0[1, j] = a.reshape(groups, sub, cols)
            return 0

        lax.fori_loop(0, depth // 2, turn, 0)
        turned = mirror(halo_m[1].reshape(depth * sub, cols)).reshape(depth, sub, cols)
        for i in range(depth):
            halo_m[1, i] = turned[depth - 1 - i]

    def row0(r, g):
        if r < depth:
            return halo0[0, r, g]
        if r < end:
            return all_ref[r - depth, g]
        return halo0[1, r - end, g]

    def row_m(r):
        if r < depth:
            return halo_m[0, r]
        if r < end:
            return misc_ref[r - depth]
        return halo_m[1, r - end]

    def pack0(g, _):
        for k in range(packs):
            send0[0, g, k], send0[1, g, k] = packed(lambda p: row0(k * per + p, g))
        return 0

    lax.fori_loop(0, groups, pack0, 0)
    for k in range(packs):
        send0[0, groups, k], send0[1, groups, k] = packed(lambda p: row_m(k * per + p))
    go_e = remote(send0.at[0], recv0.at[0], col0_send.at[0], col0_recv.at[0], east)
    go_w = remote(send0.at[1], recv0.at[1], col0_send.at[1], col0_recv.at[1], west)
    go_e.start()
    go_w.start()

    def weights(tile, get, get_m):
        def fields(c, _):
            for r in range(tall):
                mask = jnp.broadcast_to(get_m(r)[2:3], (sub, cols))
                u, v, k = get(r, c * 5 + 2), get(r, c * 5 + 3), get(r, c * 5 + 4)
                w = mask * (jnp.maximum(u, 0.0) + k)
                e = mask * (jnp.maximum(-u, 0.0) + k)
                s = mask * (jnp.maximum(v, 0.0) + k)
                if r == depth:
                    s = jnp.where(pos == 0, 0.0, 1.0) * s
                n = mask * (jnp.maximum(-v, 0.0) + k)
                coef[c, tile, r, 0] = 1.0 - ((w + e) + (s + n))
                coef[c, tile, r, 1] = w
                coef[c, tile, r, 2] = e
                coef[c, tile, r, 3] = s
                coef[c, tile, r, 4] = n
            return 0

        lax.fori_loop(0, chunks, fields, 0)
        level = lax.broadcasted_iota(jnp.int32, (sub, cols), 0)
        for r in range(tall):
            misc = get_m(r)
            for t in range(2):
                force[t, tile, r] = jnp.where(level == 0, misc[2:3] * misc[t : t + 1], 0.0)

    weights(0, row0, row_m)
    go_e.wait()
    go_w.wait()

    def unpack0(g, _):
        for k in range(packs):
            from_w, from_e = recv0[0, g, k], recv0[1, g, k]
            for p in range(per):
                xt0[k * per + p, g] = unpacked(from_w, from_e, p)
        return 0

    lax.fori_loop(0, groups + 1, unpack0, 0)
    weights(1, lambda r, g: xt0[r, g], lambda r: xt0[r, groups])

    def chunk_rows(e, c):
        return row_copies(
            st.at[pl.ds(rows - depth, depth), pl.ds(2 * c, 2)],
            st.at[pl.ds(0, depth), pl.ds(2 * c, 2)],
            lambda s: halo1.at[e, c, s], lambda s: row_send.at[e, c, s], lambda s: row_recv.at[e, c, s],
        )

    def chunk_cols(e, c):
        return (
            remote(send1.at[e, c, 0], recv1.at[e, c, 0], col_send.at[e, c, 0], col_recv.at[e, c, 0], east),
            remote(send1.at[e, c, 1], recv1.at[e, c, 1], col_send.at[e, c, 1], col_recv.at[e, c, 1], west),
        )

    def row1(e, c, r, t):
        if r < depth:
            return halo1[e, c, 0, r, t]
        if r < end:
            return st[r - depth, 2 * c + t]
        return halo1[e, c, 1, r - end, t]

    def pass_on(e, c):
        finish(chunk_rows(e, c))

        @pl.when(top)
        def _():
            whole = halo1[e, c, 1].reshape(depth * 2 * sub, cols)
            turned = mirror(whole).reshape(depth, 2, sub, cols)
            for i in range(depth):
                halo1[e, c, 1, i] = turned[depth - 1 - i]

        for t in range(2):
            for k in range(packs):
                to_east, to_west = packed(lambda p: row1(e, c, k * per + p, t))
                send1[e, c, 0, t, k] = to_east
                send1[e, c, 1, t, k] = to_west
        for copy in chunk_cols(e, c):
            copy.start()

    def collect(e, c):
        for copy in chunk_cols(e, c):
            copy.wait()
        for t in range(2):
            for k in range(packs):
                from_w, from_e = recv1[e, c, 0, t, k], recv1[e, c, 1, t, k]
                for p in range(per):
                    ping[1, k * per + p, t] = unpacked(from_w, from_e, p)
            for r in range(tall):
                ping[0, r, t] = row1(e, c, r, t)

    def steps(c):
        for s in range(depth):
            src, dst = (ping, pong) if s % 2 == 0 else (pong, ping)
            done = s == depth - 1
            for r in range(s + 1, tall - 1 - s):
                for t in range(2):
                    centre, extra = src[0, r, t], src[1, r, t]
                    rc, rx = pltpu.roll(centre, 1, 1), pltpu.roll(extra, 1, 1)
                    lc, lx = pltpu.roll(centre, cols - 1, 1), pltpu.roll(extra, cols - 1, 1)
                    tiles = (
                        (centre, jnp.where(first, rx, rc), jnp.where(final, lx, lc)),
                        (extra, jnp.where(first, rc, rx), jnp.where(final, lc, lx)),
                    )
                    for i, (mine, w, e) in enumerate(tiles[:1] if done else tiles):
                        new = coef[c, i, r, 0] * mine + (coef[c, i, r, 1] * w + coef[c, i, r, 2] * e)
                        new = new + (
                            coef[c, i, r, 3] * src[i, r - 1, t] + coef[c, i, r, 4] * src[i, r + 1, t]
                        )
                        if done:
                            st[r - depth, 2 * c + t] = new
                        else:
                            dst[i, r, t] = new

            @pl.when(c == 0)
            def _():
                for r in range(s + 1, tall - 1 - s):
                    for t in range(2):
                        if done:
                            st[r - depth, t] += force[t, 0, r]
                        else:
                            dst[0, r, t] += force[t, 0, r]
                            dst[1, r, t] += force[t, 1, r]

    def item(i, _):
        e, c = i // chunks, i % chunks

        @pl.when(e == 0)
        def _():
            for r in range(tall):
                for t in range(2):
                    ping[0, r, t] = row0(r, c * 5 + t)
                    ping[1, r, t] = xt0[r, c * 5 + t]

        @pl.when(e > 0)
        def _():
            collect(e - 1, c)

        steps(c)

        @pl.when(e < rounds - 1)
        def _():
            begin(chunk_rows(e, c))

        j = i - 1

        @pl.when(jnp.logical_and(j >= 0, j < (rounds - 1) * chunks))
        def _():
            pass_on(j // chunks, j % chunks)

        return 0

    lax.fori_loop(0, rounds * chunks, item, 0)


def ocean(fields, misc):
    rows, groups, sub, cols = fields.shape
    chunks = groups // 5
    depth = DEPTH
    tall = rows + 2 * depth
    packs = tall * depth // cols
    later = ITERS // depth - 1
    vm = lambda *shape: pltpu.VMEM((*shape, sub, cols), F32)
    dma = lambda *shape: pltpu.SemaphoreType.DMA(shape)
    return pl.pallas_call(
        functools.partial(
            ocean_kernel, face_count=lax.axis_size("face"),
            gy_count=lax.axis_size("gy"), gx_count=lax.axis_size("gx"),
        ),
        in_specs=[pl.BlockSpec(memory_space=pltpu.VMEM)] * 2,
        out_specs=pl.BlockSpec(memory_space=pltpu.VMEM),
        out_shape=jax.ShapeDtypeStruct((rows, 2 * chunks, sub, cols), F32),
        scratch_shapes=[
            vm(2, depth, groups),
            vm(2, depth),
            vm(later, chunks, 2, depth, 2),
            vm(2, groups + 1, packs),
            vm(2, groups + 1, packs),
            vm(later, chunks, 2, 2, packs),
            vm(later, chunks, 2, 2, packs),
            vm(tall, groups + 1),
            vm(2, tall, 2),
            vm(2, tall, 2),
            vm(chunks, 2, tall, 5),
            vm(2, 2, tall),
            dma(2), dma(2), dma(2), dma(2), dma(2), dma(2),
            dma(later, chunks, 2), dma(later, chunks, 2), dma(later, chunks, 2), dma(later, chunks, 2),
        ],
        compiler_params=pltpu.CompilerParams(
            collective_id=0, has_side_effects=True, vmem_limit_bytes=48 * 1024 * 1024
        ),
        name="ocean",
    )(fields, misc)


def shifted(value, axis, step, wrap):
    count = lax.axis_size(axis)
    pairs = [(i, (i + step) % count) for i in range(count) if wrap or 0 <= i + step < count]
    return lax.ppermute(value, axis, pairs)


def local(
    atmos_state, atmos_kappa, ocean_tracers, ocean_flow, ocean_kappa, sea_mask,
    xgrid_atmos_cell, xgrid_ocean_cell, xgrid_weights,
):
    rows, cols = ocean_tracers.shape[2], ocean_tracers.shape[3]
    slots = xgrid_atmos_cell.shape[2]
    lat = ("face", "gy")
    lowest = atmos_state[:, 0].reshape(-1, cols)
    surface = jnp.concatenate(
        [ocean_tracers[0, 0], current_scale * ocean_flow[0, 0], current_scale * ocean_flow[1, 0]]
    )[None]
    tall = jnp.concatenate(
        [shifted(surface, lat, 1, False), surface, shifted(surface, lat, -1, False)]
    )
    nearby = jnp.stack([shifted(tall, "gx", 1, True), tall, shifted(tall, "gx", -1, True)], axis=1)
    atmos_flux, blocks = xgrid(
        lowest,
        nearby.reshape(9, 3 * rows, cols),
        xgrid_atmos_cell.reshape(9, 1, slots),
        xgrid_ocean_cell.reshape(9, 1, slots),
        xgrid_weights.reshape(2, 9, 1, slots),
        rows, cols,
    )
    blocks = blocks.reshape(3, 3, 4, rows, cols)
    middle = (
        blocks[1] + shifted(blocks[2], lat, 1, False) + shifted(blocks[0], lat, -1, False)
    )
    ocean_flux = (
        middle[1] + shifted(middle[2], "gx", 1, True) + shifted(middle[0], "gx", -1, True)
    )
    atmos_now = atmosphere(atmos_state, atmos_kappa, atmos_flux.reshape(4, rows, cols))
    sea_weight = sea_mask.astype(F32)
    levels = ocean_tracers.shape[1]
    fields = jnp.concatenate([ocean_tracers, ocean_flow, ocean_kappa[None]])
    fields = fields.reshape(5, levels // 8, 8, rows, cols).transpose(3, 1, 0, 2, 4)
    fields = fields.reshape(rows, 5 * levels // 8, 8, cols)
    forcing = jnp.stack(
        [-ocean_gain * (ocean_flux[0] + ocean_flux[1]), ocean_gain * ocean_flux[1], sea_weight], axis=1
    )
    misc = jnp.pad(forcing, ((0, 0), (0, 5), (0, 0)))
    ocean_now = ocean(fields, misc).reshape(rows, levels // 8, 2, 8, cols)
    ocean_now = ocean_now.transpose(2, 1, 3, 0, 4).reshape(ocean_tracers.shape)
    return (atmos_now, ocean_now, sea_weight * ocean_flux[2:4])


def solution(mesh):
    placed = (
        P(None, None, ("face", "gy"), "gx"),
        P(("face", "gy"), "gx"),
        P(None, None, ("face", "gy"), "gx"),
        P(None, None, ("face", "gy"), "gx"),
        P(None, ("face", "gy"), "gx"),
        P(("face", "gy"), "gx"),
        P(("face", "gy"), "gx", None),
        P(("face", "gy"), "gx", None),
        P(None, ("face", "gy"), "gx", None),
    )
    return jax.shard_map(
        local,
        mesh=mesh,
        in_specs=placed,
        out_specs=(
            P(None, None, ("face", "gy"), "gx"),
            P(None, None, ("face", "gy"), "gx"),
            P(None, ("face", "gy"), "gx"),
        ),
        check_vma=False,
    )
```

```python
import functools

import jax
import jax.numpy as jnp
from jax import lax
from jax.experimental import pallas as pl
from jax.experimental.pallas import tpu as pltpu
from jax.sharding import PartitionSpec as P

ITERS = 24
ATM_SUB = 4
DEPTH = 8

current_scale = 2.0
atmos_gain = 0.5
ocean_gain = 0.02
MESH = pl.DeviceIdType.MESH
F32 = jnp.float32
BF16 = jnp.bfloat16


def bulk_fluxes(air_vals, sea_vals):
    temp_air, humid_air, wind_east, wind_north = air_vals
    sea_temp, current_east, current_north = sea_vals
    shear_east = wind_east - current_east
    shear_north = wind_north - current_north
    wind_speed = jnp.sqrt(shear_east * shear_east + shear_north * shear_north + 0.25)
    richardson = (temp_air - sea_temp) / (wind_speed * wind_speed)
    heat_coeff = 0.1 + 0.4 * jax.nn.sigmoid(-2.0 * richardson)
    drag_coeff = 0.2 + 0.1 * jnp.tanh(wind_speed)
    sensible = heat_coeff * wind_speed * (sea_temp - temp_air)
    latent = heat_coeff * wind_speed * (0.5 * jnp.exp(0.3 * sea_temp) - humid_air)
    return [
        sensible,
        latent,
        drag_coeff * wind_speed * shear_east,
        drag_coeff * wind_speed * shear_north,
    ]


def pieces(value):
    parts = []
    for _ in range(3):
        part = value.astype(BF16)
        parts.append(part)
        value = value - part.astype(F32)
    return parts


def pick(table, onehot_col, onehot_row, rows, fields):
    total = None
    for part in pieces(table):
        term = lax.dot_general(part, onehot_col, (((1,), (0,)), ((), ())), preferred_element_type=F32)
        total = term if total is None else total + term
    return [
        jnp.sum(jnp.where(onehot_row, total[f * rows : (f + 1) * rows], 0.0), axis=0, keepdims=True)
        for f in range(fields)
    ]


def place(values, onehot_col, onehot_row):
    split = [pieces(value) for value in values]
    total = None
    for k in range(3):
        spread = jnp.concatenate(
            [jnp.where(onehot_row, part[k].astype(F32), 0.0) for part in split], axis=0
        ).astype(BF16)
        term = lax.dot_general(spread, onehot_col, (((1,), (1,)), ((), ())), preferred_element_type=F32)
        total = term if total is None else total + term
    return total


def xgrid_kernel(low_ref, near_ref, acell_ref, ocell_ref, w_ref, aflux_ref, oflux_ref, *, rows, cols):
    slots = acell_ref.shape[2]
    bits = cols.bit_length() - 1
    col_iota = lax.broadcasted_iota(jnp.int32, (cols, slots), 0)
    row_iota = lax.broadcasted_iota(jnp.int32, (rows, slots), 0)

    def hots(cell):
        col = jnp.where(col_iota == (cell & (cols - 1)), 1.0, 0.0).astype(BF16)
        return col, row_iota == (cell >> bits)

    acol, arow = hots(acell_ref[0])
    ocol, orow = hots(ocell_ref[0])
    air = pick(low_ref[...], acol, arow, rows, 4)
    sea = pick(near_ref[0], ocol, orow, rows, 3)
    fluxes = bulk_fluxes(air, sea)
    weight_air = w_ref[0, 0]
    weight_sea = w_ref[1, 0]
    mine = place([weight_air * flux for flux in fluxes], acol, arow)

    @pl.when(pl.program_id(0) == 0)
    def _():
        aflux_ref[...] = mine

    @pl.when(pl.program_id(0) > 0)
    def _():
        aflux_ref[...] += mine

    oflux_ref[0] = place([weight_sea * flux for flux in fluxes], ocol, orow)


def xgrid(lowest, nearby, acell, ocell, weights, rows, cols):
    count, _, slots = acell.shape
    return pl.pallas_call(
        functools.partial(xgrid_kernel, rows=rows, cols=cols),
        grid=(count,),
        in_specs=[
            pl.BlockSpec((4 * rows, cols), lambda j: (0, 0)),
            pl.BlockSpec((1, 3 * rows, cols), lambda j: (j, 0, 0)),
            pl.BlockSpec((1, 1, slots), lambda j: (j, 0, 0)),
            pl.BlockSpec((1, 1, slots), lambda j: (j, 0, 0)),
            pl.BlockSpec((2, 1, 1, slots), lambda j: (0, j, 0, 0)),
        ],
        out_specs=[
            pl.BlockSpec((4 * rows, cols), lambda j: (0, 0)),
            pl.BlockSpec((1, 4 * rows, cols), lambda j: (j, 0, 0)),
        ],
        out_shape=[
            jax.ShapeDtypeStruct((4 * rows, cols), F32),
            jax.ShapeDtypeStruct((count, 4 * rows, cols), F32),
        ],
        name="xgrid",
    )(lowest, nearby, acell, ocell, weights)


def atmos_kernel(state_ref, kappa_ref, flux_ref, out_ref):
    levels, rows = state_ref.shape[1], state_ref.shape[2]
    gain = jnp.where(pl.program_id(0) < 2, atmos_gain, -atmos_gain)
    for tile in range(rows // 8):
        at = slice(tile * 8, tile * 8 + 8)
        kappa = kappa_ref[at, :]
        now = [state_ref[0, level, at, :] for level in range(levels)]
        now[0] = now[0] + gain * flux_ref[0, at, :]
        for _ in range(ATM_SUB):
            now = [
                now[l] + kappa * (now[min(l + 1, levels - 1)] + now[max(l - 1, 0)] - 2.0 * now[l])
                for l in range(levels)
            ]
        for level in range(levels):
            out_ref[0, level, at, :] = now[level]


def atmosphere(state, kappa, flux):
    fields, levels, rows, cols = state.shape
    return pl.pallas_call(
        atmos_kernel,
        grid=(fields,),
        in_specs=[
            pl.BlockSpec((1, levels, rows, cols), lambda f: (f, 0, 0, 0)),
            pl.BlockSpec((rows, cols), lambda f: (0, 0)),
            pl.BlockSpec((1, rows, cols), lambda f: (f, 0, 0)),
        ],
        out_specs=pl.BlockSpec((1, levels, rows, cols), lambda f: (f, 0, 0, 0)),
        out_shape=jax.ShapeDtypeStruct(state.shape, F32),
        name="atmosphere",
    )(state, kappa, flux)


def mirror(value):
    cols = value.shape[1]
    row = lax.broadcasted_iota(jnp.int32, (cols, cols), 0)
    col = lax.broadcasted_iota(jnp.int32, (cols, cols), 1)
    swap = jnp.where(row + col == cols - 1, 1.0, 0.0).astype(BF16)
    total = None
    for part in pieces(value):
        term = jnp.dot(part, swap, preferred_element_type=F32)
        total = term if total is None else total + term
    return total


def ocean_kernel(
    all_ref, misc_ref, edge_ref, st,
    halo0, halo_m, halo1, send0, recv0, send1, recv1, xt0, ping, pong, coef, force,
    misc_send, misc_recv, col0_send, col0_recv,
    row_send, row_recv, col_send, col_recv,
    *, face_count, gy_count, gx_count,
):
    rows, groups, sub, cols = all_ref.shape
    chunks = groups // 5
    depth = DEPTH
    tall = rows + 2 * depth
    per = cols // depth
    packs = tall // per
    rounds = ITERS // depth
    end = depth + rows

    face, gy, gx = lax.axis_index("face"), lax.axis_index("gy"), lax.axis_index("gx")
    pos = face * gy_count + gy
    last = face_count * gy_count - 1
    top = pos == last
    n_pos = jnp.where(top, pos, pos + 1)
    n_gx = jnp.where(top, gx_count - 1 - gx, gx)
    s_pos = jnp.where(pos > 0, pos - 1, 0)
    north = {"face": n_pos // gy_count, "gx": n_gx, "gy": n_pos % gy_count}
    south = {"face": s_pos // gy_count, "gx": gx, "gy": s_pos % gy_count}
    east = {"face": face, "gx": (gx + 1) % gx_count, "gy": gy}
    west = {"face": face, "gx": (gx + gx_count - 1) % gx_count, "gy": gy}
    n_slot = jnp.where(top, 1, 0)

    barrier = pltpu.get_barrier_semaphore()
    for where in (north, east, west):
        pl.semaphore_signal(barrier, inc=1, device_id=where, device_id_type=MESH)

    @pl.when(pos > 0)
    def _():
        pl.semaphore_signal(barrier, inc=1, device_id=south, device_id_type=MESH)

    @pl.when(pos == 0)
    def _():
        def clear(r, _):
            halo_m[0, r] = jnp.zeros((sub, cols), F32)
            for e in range(rounds - 1):
                for c in range(chunks):
                    halo1[e, c, 0, r] = jnp.zeros((2, sub, cols), F32)
            return 0

        lax.fori_loop(0, depth, clear, 0)

    pl.semaphore_wait(barrier, jnp.where(pos > 0, 4, 3))

    def remote(src, dst, send, recv, device):
        return pltpu.make_async_remote_copy(
            src_ref=src, dst_ref=dst, send_sem=send, recv_sem=recv,
            device_id=device, device_id_type=MESH,
        )

    def row_copies(high, low, halo_of, send, recv):
        up = remote(high, halo_of(n_slot), send(0), recv(n_slot), north)
        down = remote(low, halo_of(1), send(1), recv(1), south)
        below = remote(low, halo_of(0), send(1), recv(0), south)
        return up, down, below

    def begin(copies):
        copies[0].start()

        @pl.when(pos > 0)
        def _():
            copies[1].start()

    def finish(copies):
        up, down, below = copies

        @pl.when(pos > 0)
        def _():
            below.wait_recv()
            down.wait_send()

        down.wait_recv()
        up.wait_send()

    lane = lax.broadcasted_iota(jnp.int32, (sub, cols), 1)
    slot = lane // depth

    def packed(value_of):
        to_east, to_west = None, None
        for p in range(per):
            value = value_of(p)
            shift_e = (p + 1) * depth % cols
            moved_e = pltpu.roll(value, shift_e, 1) if shift_e else value
            moved_w = pltpu.roll(value, p * depth, 1) if p else value
            to_east = moved_e if p == 0 else jnp.where(slot == p, moved_e, to_east)
            to_west = moved_w if p == 0 else jnp.where(slot == p, moved_w, to_west)
        return to_east, to_west

    def unpacked(from_w, from_e, p):
        shift_w = (cols - depth - p * depth) % cols
        low = pltpu.roll(from_e, cols - p * depth, 1) if p else from_e
        high = pltpu.roll(from_w, shift_w, 1) if shift_w else from_w
        return jnp.where(slot == 0, low, jnp.where(slot == per - 1, high, 0.0))

    rows_m = row_copies(
        misc_ref.at[pl.ds(rows - depth, depth)], misc_ref.at[pl.ds(0, depth)],
        lambda s: halo_m.at[s], lambda s: misc_send.at[s], lambda s: misc_recv.at[s],
    )
    begin(rows_m)

    def take(r, _):
        halo0[0, r] = edge_ref[0, r]
        halo0[1, r] = edge_ref[1, r]
        return 0

    lax.fori_loop(0, depth, take, 0)
    finish(rows_m)

    @pl.when(top)
    def _():
        kind = (lax.broadcasted_iota(jnp.int32, (groups * sub, cols), 0) // sub) % 5
        sign = jnp.where(jnp.logical_or(kind == 2, kind == 3), -1.0, 1.0)

        def turn(i, _):
            j = depth - 1 - i
            a = mirror(halo0[1, i].reshape(groups * sub, cols)) * sign
            b = mirror(halo0[1, j].reshape(groups * sub, cols)) * sign
            halo0[1, i] = b.reshape(groups, sub, cols)
            halo0[1, j] = a.reshape(groups, sub, cols)
            return 0

        lax.fori_loop(0, depth // 2, turn, 0)
        turned = mirror(halo_m[1].reshape(depth * sub, cols)).reshape(depth, sub, cols)
        for i in range(depth):
            halo_m[1, i] = turned[depth - 1 - i]

    def row0(r, g):
        if r < depth:
            return halo0[0, r, g]
        if r < end:
            return all_ref[r - depth, g]
        return halo0[1, r - end, g]

    def row_m(r):
        if r < depth:
            return halo_m[0, r]
        if r < end:
            return misc_ref[r - depth]
        return halo_m[1, r - end]

    def pack0(g, _):
        for k in range(packs):
            send0[0, g, k], send0[1, g, k] = packed(lambda p: row0(k * per + p, g))
        return 0

    lax.fori_loop(0, groups, pack0, 0)
    for k in range(packs):
        send0[0, groups, k], send0[1, groups, k] = packed(lambda p: row_m(k * per + p))
    go_e = remote(send0.at[0], recv0.at[0], col0_send.at[0], col0_recv.at[0], east)
    go_w = remote(send0.at[1], recv0.at[1], col0_send.at[1], col0_recv.at[1], west)
    go_e.start()
    go_w.start()

    def weights(tile, get, get_m):
        def fields(c, _):
            for r in range(tall):
                mask = jnp.broadcast_to(get_m(r)[2:3], (sub, cols))
                u, v, k = get(r, c * 5 + 2), get(r, c * 5 + 3), get(r, c * 5 + 4)
                w = mask * (jnp.maximum(u, 0.0) + k)
                e = mask * (jnp.maximum(-u, 0.0) + k)
                s = mask * (jnp.maximum(v, 0.0) + k)
                if r == depth:
                    s = jnp.where(pos == 0, 0.0, 1.0) * s
                n = mask * (jnp.maximum(-v, 0.0) + k)
                coef[c, tile, r, 0] = 1.0 - ((w + e) + (s + n))
                coef[c, tile, r, 1] = w
                coef[c, tile, r, 2] = e
                coef[c, tile, r, 3] = s
                coef[c, tile, r, 4] = n
            return 0

        lax.fori_loop(0, chunks, fields, 0)
        level = lax.broadcasted_iota(jnp.int32, (sub, cols), 0)
        for r in range(tall):
            misc = get_m(r)
            for t in range(2):
                force[t, tile, r] = jnp.where(level == 0, misc[2:3] * misc[t : t + 1], 0.0)

    weights(0, row0, row_m)
    go_e.wait()
    go_w.wait()

    def unpack0(g, _):
        for k in range(packs):
            from_w, from_e = recv0[0, g, k], recv0[1, g, k]
            for p in range(per):
                xt0[k * per + p, g] = unpacked(from_w, from_e, p)
        return 0

    lax.fori_loop(0, groups + 1, unpack0, 0)
    weights(1, lambda r, g: xt0[r, g], lambda r: xt0[r, groups])

    def chunk_rows(e, c):
        return row_copies(
            st.at[pl.ds(rows - depth, depth), pl.ds(2 * c, 2)],
            st.at[pl.ds(0, depth), pl.ds(2 * c, 2)],
            lambda s: halo1.at[e, c, s], lambda s: row_send.at[e, c, s], lambda s: row_recv.at[e, c, s],
        )

    def chunk_cols(e, c):
        return (
            remote(send1.at[e, c, 0], recv1.at[e, c, 0], col_send.at[e, c, 0], col_recv.at[e, c, 0], east),
            remote(send1.at[e, c, 1], recv1.at[e, c, 1], col_send.at[e, c, 1], col_recv.at[e, c, 1], west),
        )

    def row1(e, c, r, t):
        if r < depth:
            return halo1[e, c, 0, r, t]
        if r < end:
            return st[r - depth, 2 * c + t]
        return halo1[e, c, 1, r - end, t]

    def pass_on(e, c):
        finish(chunk_rows(e, c))

        @pl.when(top)
        def _():
            whole = halo1[e, c, 1].reshape(depth * 2 * sub, cols)
            turned = mirror(whole).reshape(depth, 2, sub, cols)
            for i in range(depth):
                halo1[e, c, 1, i] = turned[depth - 1 - i]

        for t in range(2):
            for k in range(packs):
                to_east, to_west = packed(lambda p: row1(e, c, k * per + p, t))
                send1[e, c, 0, t, k] = to_east
                send1[e, c, 1, t, k] = to_west
        for copy in chunk_cols(e, c):
            copy.start()

    def collect(e, c):
        for copy in chunk_cols(e, c):
            copy.wait()
        for t in range(2):
            for k in range(packs):
                from_w, from_e = recv1[e, c, 0, t, k], recv1[e, c, 1, t, k]
                for p in range(per):
                    ping[1, k * per + p, t] = unpacked(from_w, from_e, p)
            for r in range(tall):
                ping[0, r, t] = row1(e, c, r, t)

    lane2 = lax.broadcasted_iota(jnp.int32, (2, sub, cols), 2)
    first2 = lane2 == 0
    final2 = lane2 == cols - 1

    def steps(c):
        for s in range(depth):
            src, dst = (ping, pong) if s % 2 == 0 else (pong, ping)
            done = s == depth - 1
            for r in range(s + 1, tall - 1 - s):
                centre, extra = src[0, r], src[1, r]
                rc, rx = pltpu.roll(centre, 1, 2), pltpu.roll(extra, 1, 2)
                lc, lx = pltpu.roll(centre, cols - 1, 2), pltpu.roll(extra, cols - 1, 2)
                tiles = (
                    (centre, jnp.where(first2, rx, rc), jnp.where(final2, lx, lc)),
                    (extra, jnp.where(first2, rc, rx), jnp.where(final2, lc, lx)),
                )
                for i, (mine, w, e) in enumerate(tiles[:1] if done else tiles):
                    k = coef[c, i, r]
                    new = k[0:1] * mine + (k[1:2] * w + k[2:3] * e)
                    new = new + (k[3:4] * src[i, r - 1] + k[4:5] * src[i, r + 1])
                    if done:
                        st[r - depth, pl.ds(2 * c, 2)] = new
                    else:
                        dst[i, r] = new

            @pl.when(c == 0)
            def _():
                for r in range(s + 1, tall - 1 - s):
                    for t in range(2):
                        if done:
                            st[r - depth, t] += force[t, 0, r]
                        else:
                            dst[0, r, t] += force[t, 0, r]
                            dst[1, r, t] += force[t, 1, r]

    def item(i, _):
        e, c = i // chunks, i % chunks

        @pl.when(e == 0)
        def _():
            for r in range(tall):
                for t in range(2):
                    ping[0, r, t] = row0(r, c * 5 + t)
                    ping[1, r, t] = xt0[r, c * 5 + t]

        @pl.when(e > 0)
        def _():
            collect(e - 1, c)

        steps(c)

        @pl.when(e < rounds - 1)
        def _():
            begin(chunk_rows(e, c))

        j = i - 1

        @pl.when(jnp.logical_and(j >= 0, j < (rounds - 1) * chunks))
        def _():
            pass_on(j // chunks, j % chunks)

        return 0

    lax.fori_loop(0, rounds * chunks, item, 0)


def ocean(fields, misc, edges):
    rows, groups, sub, cols = fields.shape
    chunks = groups // 5
    depth = DEPTH
    tall = rows + 2 * depth
    packs = tall * depth // cols
    later = ITERS // depth - 1
    vm = lambda *shape: pltpu.VMEM((*shape, sub, cols), F32)
    dma = lambda *shape: pltpu.SemaphoreType.DMA(shape)
    return pl.pallas_call(
        functools.partial(
            ocean_kernel, face_count=lax.axis_size("face"),
            gy_count=lax.axis_size("gy"), gx_count=lax.axis_size("gx"),
        ),
        in_specs=[pl.BlockSpec(memory_space=pltpu.VMEM)] * 3,
        out_specs=pl.BlockSpec(memory_space=pltpu.VMEM),
        out_shape=jax.ShapeDtypeStruct((rows, 2 * chunks, sub, cols), F32),
        scratch_shapes=[
            vm(2, depth, groups),
            vm(2, depth),
            vm(later, chunks, 2, depth, 2),
            vm(2, groups + 1, packs),
            vm(2, groups + 1, packs),
            vm(later, chunks, 2, 2, packs),
            vm(later, chunks, 2, 2, packs),
            vm(tall, groups + 1),
            vm(2, tall, 2),
            vm(2, tall, 2),
            vm(chunks, 2, tall, 5),
            vm(2, 2, tall),
            dma(2), dma(2), dma(2), dma(2),
            dma(later, chunks, 2), dma(later, chunks, 2), dma(later, chunks, 2), dma(later, chunks, 2),
        ],
        compiler_params=pltpu.CompilerParams(
            collective_id=0, has_side_effects=True, vmem_limit_bytes=48 * 1024 * 1024
        ),
        name="ocean",
    )(fields, misc, edges)


def shifted(value, axis, step, wrap):
    count = lax.axis_size(axis)
    pairs = [(i, (i + step) % count) for i in range(count) if wrap or 0 <= i + step < count]
    return lax.ppermute(value, axis, pairs)


def local(
    atmos_state, atmos_kappa, ocean_tracers, ocean_flow, ocean_kappa, sea_mask,
    xgrid_atmos_cell, xgrid_ocean_cell, xgrid_weights,
):
    rows, cols = ocean_tracers.shape[2], ocean_tracers.shape[3]
    slots = xgrid_atmos_cell.shape[2]
    lat = ("face", "gy")
    lowest = atmos_state[:, 0].reshape(-1, cols)
    surface = jnp.concatenate(
        [ocean_tracers[0, 0], current_scale * ocean_flow[0, 0], current_scale * ocean_flow[1, 0]]
    )[None]
    tall = jnp.concatenate(
        [shifted(surface, lat, 1, False), surface, shifted(surface, lat, -1, False)]
    )
    nearby = jnp.stack([shifted(tall, "gx", 1, True), tall, shifted(tall, "gx", -1, True)], axis=1)
    atmos_flux, blocks = xgrid(
        lowest,
        nearby.reshape(9, 3 * rows, cols),
        xgrid_atmos_cell.reshape(9, 1, slots),
        xgrid_ocean_cell.reshape(9, 1, slots),
        xgrid_weights.reshape(2, 9, 1, slots),
        rows, cols,
    )
    blocks = blocks.reshape(3, 3, 4, rows, cols)
    middle = (
        blocks[1] + shifted(blocks[2], lat, 1, False) + shifted(blocks[0], lat, -1, False)
    )
    ocean_flux = (
        middle[1] + shifted(middle[2], "gx", 1, True) + shifted(middle[0], "gx", -1, True)
    )
    atmos_now = atmosphere(atmos_state, atmos_kappa, atmos_flux.reshape(4, rows, cols))
    sea_weight = sea_mask.astype(F32)
    levels = ocean_tracers.shape[1]
    fields = jnp.concatenate([ocean_tracers, ocean_flow, ocean_kappa[None]])
    fields = fields.reshape(5, levels // 8, 8, rows, cols).transpose(3, 1, 0, 2, 4)
    fields = fields.reshape(rows, 5 * levels // 8, 8, cols)
    upper, lower = fields[rows - DEPTH :], fields[:DEPTH]
    faces, lon, span = lax.axis_size("face"), lax.axis_size("gx"), lax.axis_size("gy")
    tops = [((faces - 1) * lon + x) * span + span - 1 for x in range(lon)]
    beyond = lax.ppermute(upper, ("face", "gx", "gy"), list(zip(tops, tops[::-1])))
    beyond = beyond + shifted(lower, lat, -1, False)
    edges = jnp.stack([shifted(upper, lat, 1, False), beyond])
    forcing = jnp.stack(
        [-ocean_gain * (ocean_flux[0] + ocean_flux[1]), ocean_gain * ocean_flux[1], sea_weight], axis=1
    )
    misc = jnp.pad(forcing, ((0, 0), (0, 5), (0, 0)))
    ocean_now = ocean(fields, misc, edges).reshape(rows, levels // 8, 2, 8, cols)
    ocean_now = ocean_now.transpose(2, 1, 3, 0, 4).reshape(ocean_tracers.shape)
    return (atmos_now, ocean_now, sea_weight * ocean_flux[2:4])


def solution(mesh):
    placed = (
        P(None, None, ("face", "gy"), "gx"),
        P(("face", "gy"), "gx"),
        P(None, None, ("face", "gy"), "gx"),
        P(None, None, ("face", "gy"), "gx"),
        P(None, ("face", "gy"), "gx"),
        P(("face", "gy"), "gx"),
        P(("face", "gy"), "gx", None),
        P(("face", "gy"), "gx", None),
        P(None, ("face", "gy"), "gx", None),
    )
    return jax.shard_map(
        local,
        mesh=mesh,
        in_specs=placed,
        out_specs=(
            P(None, None, ("face", "gy"), "gx"),
            P(None, None, ("face", "gy"), "gx"),
            P(None, ("face", "gy"), "gx"),
        ),
        check_vma=False,
    )
```
